128 devices in a mesh: section: 2 (over y_hi), ctx: 16 (over y_lo, x, core), dp: 4 (over z).
Axes of the slice: x: 4, y: 4 (y_hi: 2, y_lo: 2; y = y_hi * 2 + y_lo), z: 4, core: 2. Of those that a mesh axis runs over, the one named last changes fastest.
Arguments:
- new_input: bfloat16 [2, 4, 2048, 6144], P('section', 'dp', 'ctx'), may hold values from -6 to 6
- new_query: bfloat16 [2, 4, 2048, 6144], P('section', 'dp', 'ctx'), may hold values from -6 to 6
- new_key: bfloat16 [2, 4, 2048, 6144], P('section', 'dp', 'ctx'), may hold values from -6 to 6
- new_value: bfloat16 [2, 4, 2048, 6144], P('section', 'dp', 'ctx'), may hold values from -6 to 6
- new_modality: int32 [2, 4, 2048], P('section', 'dp', 'ctx'), may hold values from 0 to 1, as said below
- old_query: bfloat16 [2, 4, 2048, 6144], P('section', 'dp', 'ctx'), may hold values from -6 to 6
- old_key: bfloat16 [2, 4, 2048, 6144], P('section', 'dp', 'ctx'), may hold values from -6 to 6
- old_value: bfloat16 [2, 4, 2048, 6144], P('section', 'dp', 'ctx'), may hold values from -6 to 6
- old_output: bfloat16 [2, 4, 2048, 6144], P('section', 'dp', 'ctx'), may hold values from -4 to 4
- old_cotangent: bfloat16 [2, 4, 2048, 6144], P('section', 'dp', 'ctx'), may hold values from -6 to 6
- old_modality: int32 [2, 4, 2048], P('section', 'dp', 'ctx'), may hold values from 0 to 1, as said below
- cross_bias: float32 [2, 48], P('section', 'ctx'), may hold values from -2 to 2
Outputs:
- next_input: bfloat16 [2, 4, 2048, 6144], P('section', 'dp', 'ctx')
- query_cotangent: bfloat16 [2, 4, 2048, 6144], P('section', 'dp', 'ctx')
- key_cotangent: bfloat16 [2, 4, 2048, 6144], P('section', 'dp', 'ctx')
- value_cotangent: bfloat16 [2, 4, 2048, 6144], P('section', 'dp', 'ctx')
- bias_cotangent: float32 [2, 48], P('section', 'ctx')
The draws below stay inside these ranges and needn't reach their ends.
Inputs may be any that keep to these rules, and one draw needn't show every extreme that they name: `new_modality`: 1 marks a trajectory token, 0 a video token. `old_modality`: 1 marks a trajectory token, 0 a video token.
All inputs are finite; a program needn't handle non-finite values.
Results may differ from the reference program's by a relative error of at most 0.0049.
Values may be sent and summed in bfloat16 or wider, within the bound.
A program may use at most 192 MiB of HBM per device.

```python
import math
import jax
import jax.numpy as jnp
from jax import lax

H = 48
DH = 128
HD = 6144
SEQ = 2048
SECTIONS = 2
REPLICAS = 4


def modality_draw(key, variant):
    drawn = jax.random.randint(jax.random.fold_in(key, 11 + variant), (SECTIONS, REPLICAS, SEQ), 0, 4)
    return (drawn == 0).astype(jnp.int32)


def row_scales(key, salt):
    return jnp.exp(jax.random.uniform(jax.random.fold_in(key, salt), (SECTIONS * REPLICAS, SEQ, 1), jnp.float32, math.log(0.3), math.log(2.0)))


def queries_keys(key, variant):
    sequences = SECTIONS * REPLICAS
    full_shape = (sequences, SEQ, HD)
    query_scale = row_scales(key, 21 + 4 * variant)
    key_scale = row_scales(key, 22 + 4 * variant)
    query_seed = jax.random.fold_in(key, 23 + 4 * variant)
    key_seed = jax.random.fold_in(key, 24 + 4 * variant)
    queries = jnp.clip(jax.random.normal(query_seed, full_shape, jnp.float32), -3.0, 3.0) * query_scale
    keys_drawn = jnp.clip(jax.random.normal(key_seed, full_shape, jnp.float32), -3.0, 3.0) * key_scale
    return (queries.reshape(SECTIONS, REPLICAS, SEQ, HD), keys_drawn.reshape(SECTIONS, REPLICAS, SEQ, HD))


def draw_new_query(key, part):
    return queries_keys(key, 0)[0].astype(jnp.bfloat16)


def draw_new_key(key, part):
    return queries_keys(key, 0)[1].astype(jnp.bfloat16)


def draw_new_modality(key, part):
    return modality_draw(key, 0)


def draw_old_query(key, part):
    return queries_keys(key, 1)[0].astype(jnp.bfloat16)


def draw_old_key(key, part):
    return queries_keys(key, 1)[1].astype(jnp.bfloat16)


def draw_old_modality(key, part):
    return modality_draw(key, 1)


def block_scale(stream_key, extent, cuts, smallest, largest):
    gain, own = 1.0, jax.random.fold_in(stream_key, 6)
    for dim, blocks in cuts:
        draws = jnp.exp(jax.random.uniform(jax.random.fold_in(own, dim), (blocks,), jnp.float32, smallest / len(cuts), largest / len(cuts)))
        gain = gain * jnp.repeat(draws, extent[dim] // blocks).reshape([-1 if axis == dim else 1 for axis in range(len(extent))])
    return gain


def normal_values(rng, extent, scale, reach, cuts=(), kind=jnp.bfloat16):
    result = jax.random.normal(rng, extent, jnp.float32) * scale
    if len(cuts) > 0:
        result = block_scale(rng, extent, cuts, -0.22, 0.18) * result
    return jnp.clip(result, min=-reach, max=reach).astype(kind)


def setup_inputs(seed: int = 0) -> dict:
    key_list = jax.random.split(jax.random.key(seed), 13)
    return {
        "new_input": normal_values(key_list[0], (SECTIONS, REPLICAS, SEQ, HD), 1.0, 6.0, ((0, 2), (1, 4), (2, 16))),
        "new_query": draw_new_query(jax.random.fold_in(key_list[12], 71), 0),
        "new_key": draw_new_key(jax.random.fold_in(key_list[12], 71), 0),
        "new_value": normal_values(key_list[3], (SECTIONS, REPLICAS, SEQ, HD), 1.0, 6.0, ((0, 2), (1, 4), (2, 16))),
        "new_modality": draw_new_modality(jax.random.fold_in(key_list[12], 71), 0),
        "old_query": draw_old_query(jax.random.fold_in(key_list[12], 71), 0),
        "old_key": draw_old_key(jax.random.fold_in(key_list[12], 71), 0),
        "old_value": normal_values(key_list[7], (SECTIONS, REPLICAS, SEQ, HD), 1.0, 6.0, ((0, 2), (1, 4), (2, 16))),
        "old_output": normal_values(key_list[8], (SECTIONS, REPLICAS, SEQ, HD), 0.5, 4.0, ((0, 2), (1, 4), (2, 16))),
        "old_cotangent": normal_values(key_list[9], (SECTIONS, REPLICAS, SEQ, HD), 1.0, 6.0, ((0, 2), (1, 4), (2, 16))),
        "old_modality": draw_old_modality(jax.random.fold_in(key_list[12], 71), 0),
        "cross_bias": jnp.clip(jax.random.uniform(key_list[11], (SECTIONS, H), jnp.float32, -2.0, 2.0) * block_scale(key_list[11], (SECTIONS, H), ((0, 2), (1, 16)), -0.4, 0.0), -2.0, 2.0),
    }


def head_weights(queries, keys, modality, bias_value):
    scores = jnp.dot(queries, keys.T, preferred_element_type=jnp.float32) * (DH ** -0.5)
    trajectory_rows = modality[:, None] == 1
    video_cols = modality[None, :] == 0
    crossing = (trajectory_rows & video_cols).astype(jnp.float32)
    scores = scores + bias_value * crossing
    scores = jnp.where(trajectory_rows | video_cols, scores, -jnp.inf)
    highest = jnp.max(scores, axis=1, keepdims=True)
    weights = jnp.exp(scores - highest)
    return weights / jnp.sum(weights, axis=1, keepdims=True), crossing


def columns(matrix, head_index):
    return lax.dynamic_slice_in_dim(matrix, head_index * DH, DH, 1)


def regroup(stacked):
    return jnp.transpose(stacked, (1, 0, 2)).reshape(SEQ, HD)


def forward_sequence(inputs):
    queries, keys, values, modality, biases = inputs

    def one_head(head_index):
        weights, unused = head_weights(columns(queries, head_index), columns(keys, head_index), modality, biases[head_index])
        return jnp.dot(weights.astype(jnp.bfloat16), columns(values, head_index), preferred_element_type=jnp.float32).astype(jnp.bfloat16)

    return regroup(lax.map(one_head, jnp.arange(H, dtype=jnp.int32)))


def backward_sequence(inputs):
    queries, keys, values, outputs, upstream, modality, biases = inputs
    delta_all = jnp.sum((upstream.astype(jnp.float32) * outputs.astype(jnp.float32)).reshape(SEQ, H, DH), axis=2)

    def one_head(head_index):
        query_cols = columns(queries, head_index)
        key_cols = columns(keys, head_index)
        value_cols = columns(values, head_index)
        upstream_cols = columns(upstream, head_index)
        weights, crossing = head_weights(query_cols, key_cols, modality, biases[head_index])
        value_back = jnp.dot(weights.astype(jnp.bfloat16).T, upstream_cols, preferred_element_type=jnp.float32).astype(jnp.bfloat16)
        weight_sens = jnp.dot(upstream_cols, value_cols.T, preferred_element_type=jnp.float32)
        delta_col = lax.dynamic_slice_in_dim(delta_all, head_index, 1, 1)
        score_sens = weights * (weight_sens - delta_col)
        bias_back = jnp.sum(score_sens * crossing)
        rounded = score_sens.astype(jnp.bfloat16)
        query_back = (jnp.dot(rounded, key_cols, preferred_element_type=jnp.float32) * (DH ** -0.5)).astype(jnp.bfloat16)
        key_back = (jnp.dot(rounded.T, query_cols, preferred_element_type=jnp.float32) * (DH ** -0.5)).astype(jnp.bfloat16)
        return query_back, key_back, value_back, bias_back

    query_back, key_back, value_back, bias_back = lax.map(one_head, jnp.arange(H, dtype=jnp.int32))
    return regroup(query_back), regroup(key_back), regroup(value_back), bias_back


def reference(new_input, new_query, new_key, new_value, new_modality, old_query, old_key, old_value, old_output, old_cotangent, old_modality, cross_bias):
    def flatten(tensor):
        return tensor.reshape((SECTIONS * REPLICAS,) + tensor.shape[2:])

    bias_rows = jnp.repeat(cross_bias, REPLICAS, axis=0)
    attended = lax.map(forward_sequence, (flatten(new_query), flatten(new_key), flatten(new_value), flatten(new_modality), bias_rows))
    summed = (flatten(new_input).astype(jnp.float32) + attended.astype(jnp.float32)).astype(jnp.bfloat16)
    next_input = jnp.roll(summed.reshape(new_input.shape), 1, axis=0)
    query_back, key_back, value_back, bias_back = lax.map(backward_sequence, (flatten(old_query), flatten(old_key), flatten(old_value), flatten(old_output), flatten(old_cotangent), flatten(old_modality), bias_rows))
    full_shape = new_input.shape
    bias_cotangent = jnp.sum(bias_back.reshape(SECTIONS, REPLICAS, H), axis=1)
    return next_input, query_back.reshape(full_shape), key_back.reshape(full_shape), value_back.reshape(full_shape), bias_cotangent
```

```python
import functools

import jax
import jax.numpy as jnp
from jax import lax
from jax.experimental import pallas as pl
from jax.experimental.pallas import tpu as pltpu
from jax.sharding import PartitionSpec as P

MESH = pl.DeviceIdType.MESH
NT = (((1,), (1,)), ((), ()))
TN = (((0,), (0,)), ((), ()))
F32 = jnp.float32
BF16 = jnp.bfloat16
NEG = -1e30
LOG2E = 1.4426950408889634
LANES = 128


def forward_block(i, bq, q_ref, k_ref, v_ref, o_ref, row_ref, col_ref, bias):
    length, width = k_ref.shape
    c1 = width**-0.5 * LOG2E
    rows = pl.ds(pl.multiple_of(i * bq, bq), bq)
    scores = lax.dot_general(q_ref[rows, :], k_ref[...], NT, preferred_element_type=F32)
    traj = col_ref[rows, :] > 0.5
    logits, top = [], None
    for c in range(length // LANES):
        cols = slice(c * LANES, (c + 1) * LANES)
        key_traj = row_ref[:, cols]
        yes = (1.0 - key_traj) * (bias * LOG2E)
        no = key_traj * NEG
        x = scores[:, cols] * c1 + jnp.where(traj, yes, no)
        logits.append(x)
        top = x if top is None else jnp.maximum(top, x)
    top = jnp.max(top, axis=1, keepdims=True)
    total, weights = None, []
    for x in logits:
        p = jnp.exp2(x - top)
        total = p if total is None else total + p
        weights.append(p.astype(BF16))
    total = jnp.sum(total, axis=1, keepdims=True)
    out = jnp.dot(jnp.concatenate(weights, axis=1), v_ref[...], preferred_element_type=F32)
    o_ref[rows, :] = (out / total).astype(BF16)


def backward_block(
    i, bq, bk, q_ref, k_ref, v_ref, do_ref, dq_ref, dk_acc, dv_acc, x_scr, ds_scr, b_acc, row_ref, col_ref, del_ref, bias
):
    length, width = k_ref.shape
    scale = width**-0.5
    c1 = scale * LOG2E
    rows = pl.ds(pl.multiple_of(i * bq, bq), bq)
    q = q_ref[rows, :]
    do = do_ref[rows, :]
    traj = row_ref[:, rows]
    yes = traj * (bias * LOG2E)
    no = (1.0 - traj) * NEG
    delta = del_ref[:, rows]
    blocks = [slice(c * bk, (c + 1) * bk) for c in range(length // bk)]

    def video(ks):
        return jnp.concatenate([col_ref[ks, :]] * (bq // LANES), axis=1) < 0.5

    def fold(x):
        return x.reshape(bk // 8, 8, bq)

    top = None
    for ks in blocks:
        s = lax.dot_general(k_ref[ks, :], q, NT, preferred_element_type=F32)
        x = s * c1 + jnp.where(video(ks), yes, no)
        x_scr[ks, :] = x
        t = jnp.max(fold(x), axis=0)
        top = t if top is None else jnp.maximum(top, t)
    top = jnp.max(top, axis=0, keepdims=True)
    total = None
    for ks in blocks:
        p = jnp.exp2(x_scr[ks, :] - top)
        x_scr[ks, :] = p
        t = jnp.sum(fold(p), axis=0)
        total = t if total is None else total + t
    inverse = 1.0 / jnp.sum(total, axis=0, keepdims=True)
    b_sum = None
    for ks in blocks:
        dp = lax.dot_general(v_ref[ks, :], do, NT, preferred_element_type=F32)
        p = x_scr[ks, :] * inverse
        ds = p * (dp - delta)
        t = jnp.sum(fold(jnp.where(video(ks), ds, 0.0)), axis=0)
        b_sum = t if b_sum is None else b_sum + t
        low = ds.astype(BF16)
        ds_scr[ks, :] = low
        dv_acc[ks, :] += jnp.dot(p.astype(BF16), do, preferred_element_type=F32)
        dk_acc[ks, :] += jnp.dot(low, q, preferred_element_type=F32)
    b_acc[...] += b_sum * traj
    dq = lax.dot_general(ds_scr[...], k_ref[...], TN, preferred_element_type=F32)
    dq_ref[rows, :] = (dq * scale).astype(BF16)


def body(
    heads, bqf, bq, bk,
    ni, nq, nk, nv, oq, ok, ov, oo, oc, nm, om, bias,
    att_out, ni_out, dq_out, dk_out, dv_out, db_out,
    new_buf, old_buf, att, grads, dk_acc, dv_acc, x_scr, ds_scr, b_acc, b_row, db_s, db_r,
    mod_n, mod_o, row_n, row_o, col_n, col_o, c_buf, o_buf, del_s, del_r, del_rows,
    in_recv, in_send, att_recv, att_send, ni_recv, ni_send, g_recv, g_send,
    mod_recv, mod_send, del_recv, del_send, db_recv, db_send, loc_sem,
):
    peers = lax.axis_size("ctx")
    sections = lax.axis_size("section")
    replicas = lax.axis_size("dp")
    me = lax.axis_index("ctx")
    section = lax.axis_index("section")
    replica = lax.axis_index("dp")
    next_section = (section + 1) % sections
    tokens = nq.shape[0]
    width = new_buf.shape[3]
    length = new_buf.shape[2]
    my_rows = pl.ds(pl.multiple_of(me * tokens, tokens), tokens)
    whole = pl.ds(0, (peers - 1) * tokens)

    def head_cols(p, h):
        return pl.ds(pl.multiple_of((p * heads + h) * width, width), width)

    def token_rows(p):
        return pl.ds(pl.multiple_of(p * tokens, tokens), tokens)

    barrier = pltpu.get_barrier_semaphore()

    @pl.loop(1, peers)
    def _(k):
        pl.semaphore_signal(barrier, inc=1, device_id={"ctx": (me + k) % peers}, device_id_type=MESH)

    @pl.loop(0, peers)
    def _(k):
        pl.semaphore_signal(barrier, inc=1, device_id={"section": next_section, "ctx": k}, device_id_type=MESH)

    @pl.loop(1, replicas)
    def _(k):
        pl.semaphore_signal(barrier, inc=1, device_id={"dp": (replica + k) % replicas}, device_id_type=MESH)

    pl.semaphore_wait(barrier, 2 * peers - 1 + replicas - 1)

    load_c = pltpu.make_async_copy(oc, c_buf, loc_sem.at[0])
    load_o = pltpu.make_async_copy(oo, o_buf, loc_sem.at[1])
    for ref, buf, j in ((nm, mod_n, 0), (om, mod_o, 1)):
        pltpu.make_async_copy(ref, buf.at[me], mod_recv.at[j]).start()

        @pl.loop(1, peers)
        def _(k):
            pltpu.make_async_remote_copy(
                src_ref=ref, dst_ref=buf.at[me], send_sem=mod_send.at[j], recv_sem=mod_recv.at[j],
                device_id={"ctx": (me + k) % peers}, device_id_type=MESH,
            ).start()

    def send_in(arrays, buf, first):
        @pl.loop(0, heads)
        def _(h):
            for a, src in enumerate(arrays):
                pltpu.make_async_copy(
                    src.at[:, head_cols(me, h)], buf.at[a, h, my_rows, :], in_recv.at[first + a, h]
                ).start()

            @pl.loop(1, peers)
            def _(k):
                t = (me + k) % peers
                for a, src in enumerate(arrays):
                    pltpu.make_async_remote_copy(
                        src_ref=src.at[:, head_cols(t, h)], dst_ref=buf.at[a, h, my_rows, :],
                        send_sem=in_send.at[first + a, h], recv_sem=in_recv.at[first + a, h],
                        device_id={"ctx": t}, device_id_type=MESH,
                    ).start()

    send_in((nq, nk, nv), new_buf, 0)
    load_c.start()
    load_o.start()
    send_in((oq, ok, ov, oc), old_buf, 3)
    ni_copy = pltpu.make_async_remote_copy(
        src_ref=ni, dst_ref=ni_out, send_sem=ni_send, recv_sem=ni_recv,
        device_id={"section": next_section}, device_id_type=MESH,
    )
    ni_copy.start()

    load_c.wait()
    load_o.wait()

    @pl.loop(0, peers)
    def _(p):
        for j in range(heads):
            cols = head_cols(p, j)
            prod = c_buf[:, cols].astype(F32) * o_buf[:, cols].astype(F32)
            del_s[p, j : j + 1, :] = jnp.sum(prod.T, axis=0, keepdims=True)

    for buf, row, col, j in ((mod_n, row_n, col_n, 0), (mod_o, row_o, col_o, 1)):
        pltpu.make_async_copy(buf, buf, mod_recv.at[j]).wait()
        for c in range(peers):
            flags = (buf[c] == 1).astype(F32)
            row[:, c * tokens : (c + 1) * tokens] = flags
            col[c * tokens : (c + 1) * tokens, :] = jnp.broadcast_to(flags, (LANES, tokens)).T

    def wait_in(buf, a, first, h):
        pltpu.make_async_copy(buf.at[a, h], buf.at[a, h], in_recv.at[first + a, h]).wait()

    @pl.loop(0, heads)
    def _(h):
        for a in range(3):
            wait_in(new_buf, a, 0, h)
        limit = bias[0, h]

        @pl.loop(0, length // bqf)
        def _(i):
            forward_block(
                i, bqf, new_buf.at[0, h], new_buf.at[1, h], new_buf.at[2, h], att.at[h], row_n, col_n, limit
            )

        @pl.loop(0, peers)
        def _(k):
            t = (me + k) % peers
            pltpu.make_async_remote_copy(
                src_ref=att.at[h, token_rows(t), :], dst_ref=att_out.at[:, head_cols(me, h)],
                send_sem=att_send.at[h], recv_sem=att_recv,
                device_id={"section": next_section, "ctx": t}, device_id_type=MESH,
            ).start()

        @pl.when(h == 0)
        def _():
            pltpu.make_async_copy(del_s.at[me], del_r.at[me], del_recv).start()

            @pl.loop(1, peers)
            def _(k):
                t = (me + k) % peers
                pltpu.make_async_remote_copy(
                    src_ref=del_s.at[t], dst_ref=del_r.at[me], send_sem=del_send, recv_sem=del_recv,
                    device_id={"ctx": t}, device_id_type=MESH,
                ).start()

    pltpu.make_async_copy(del_r, del_r, del_recv).wait()
    for c in range(peers):
        for j in range(heads):
            del_rows[j, :, c * tokens : (c + 1) * tokens] = del_r[c, j : j + 1, :]

    b_row[...] = jnp.zeros_like(b_row)
    lane = lax.broadcasted_iota(jnp.int32, (8, LANES), 1)

    @pl.loop(0, heads)
    def _(h):
        for a in range(4):
            wait_in(old_buf, a, 3, h)
        limit = bias[0, h]
        dk_acc[...] = jnp.zeros_like(dk_acc)
        dv_acc[...] = jnp.zeros_like(dv_acc)
        b_acc[...] = jnp.zeros_like(b_acc)

        @pl.loop(0, length // bq)
        def _(i):
            backward_block(
                i, bq, bk, old_buf.at[0, h], old_buf.at[1, h], old_buf.at[2, h], old_buf.at[3, h],
                grads.at[0, h], dk_acc, dv_acc, x_scr, ds_scr, b_acc, row_o, col_o, del_rows.at[h], limit,
            )

        grads[1, h] = (dk_acc[...] * width**-0.5).astype(BF16)
        grads[2, h] = dv_acc[...].astype(BF16)
        share = jnp.sum(jnp.sum(b_acc[...], axis=0, keepdims=True), axis=1, keepdims=True)
        b_row[...] += jnp.where(lane == h, share, 0.0)
        for g, out in enumerate((dq_out, dk_out, dv_out)):
            pltpu.make_async_copy(grads.at[g, h, my_rows, :], out.at[:, head_cols(me, h)], g_recv.at[g]).start()

        @pl.loop(1, peers)
        def _(k):
            t = (me + k) % peers
            for g, out in enumerate((dq_out, dk_out, dv_out)):
                pltpu.make_async_remote_copy(
                    src_ref=grads.at[g, h, token_rows(t), :], dst_ref=out.at[:, head_cols(me, h)],
                    send_sem=g_send.at[g, h], recv_sem=g_recv.at[g],
                    device_id={"ctx": t}, device_id_type=MESH,
                ).start()

    db_s[...] = b_row[...]
    pltpu.make_async_copy(db_s, db_r.at[replica], db_recv).start()

    @pl.loop(1, replicas)
    def _(k):
        pltpu.make_async_remote_copy(
            src_ref=db_s, dst_ref=db_r.at[replica], send_sem=db_send, recv_sem=db_recv,
            device_id={"dp": (replica + k) % replicas}, device_id_type=MESH,
        ).start()

    pltpu.make_async_copy(db_r, db_r, db_recv).wait()
    acc = db_r[0]
    for r in range(1, replicas):
        acc = acc + db_r[r]
    db_out[...] = acc

    def drain(ref, sem):
        pltpu.make_async_copy(ref, ref, sem).wait()

    for j, buf in enumerate((mod_n, mod_o)):
        drain(buf.at[pl.ds(0, peers - 1)], mod_send.at[j])
    drain(del_s.at[pl.ds(0, peers - 1)], del_send)
    drain(db_r.at[pl.ds(0, replicas - 1)], db_send)

    @pl.loop(0, heads)
    def _(h):
        for a in range(3):
            drain(new_buf.at[a, h, whole, :], in_send.at[a, h])
        for a in range(4):
            drain(old_buf.at[a, h, whole, :], in_send.at[3 + a, h])
        drain(att.at[h], att_send.at[h])
        for g in range(3):
            drain(grads.at[g, h, whole, :], g_send.at[g, h])

    ni_copy.wait()
    drain(att_out, att_recv)
    for g, out in enumerate((dq_out, dk_out, dv_out)):
        drain(out, g_recv.at[g])


def shards(
    new_input, new_query, new_key, new_value, new_modality,
    old_query, old_key, old_value, old_output, old_cotangent, old_modality, cross_bias,
):
    tokens, features = new_query.shape[2:]
    heads = cross_bias.shape[1]
    peers = lax.axis_size("ctx")
    replicas = lax.axis_size("dp")
    length = tokens * peers
    width = features // (heads * peers)
    bqf, bq, bk = 256, 256, 256

    def flat(x):
        return x.reshape(x.shape[-2:])

    full = jax.ShapeDtypeStruct((tokens, features), BF16)
    dma = pltpu.SemaphoreType.DMA
    any_spec = pl.BlockSpec(memory_space=pl.ANY)
    att, shifted, dq, dk, dv, db = pl.pallas_call(
        functools.partial(body, heads, bqf, bq, bk),
        out_shape=[full] * 5 + [jax.ShapeDtypeStruct((8, LANES), F32)],
        in_specs=[any_spec] * 11 + [pl.BlockSpec(memory_space=pltpu.SMEM)],
        out_specs=[any_spec] * 5 + [pl.BlockSpec(memory_space=pltpu.VMEM)],
        scratch_shapes=[
            pltpu.VMEM((3, heads, length, width), BF16),
            pltpu.VMEM((4, heads, length, width), BF16),
            pltpu.VMEM((heads, length, width), BF16),
            pltpu.VMEM((3, heads, length, width), BF16),
            pltpu.VMEM((length, width), F32),
            pltpu.VMEM((length, width), F32),
            pltpu.VMEM((length, bq), F32),
            pltpu.VMEM((length, bq), BF16),
            pltpu.VMEM((8, bq), F32),
            pltpu.VMEM((8, LANES), F32),
            pltpu.VMEM((8, LANES), F32),
            pltpu.VMEM((replicas, 8, LANES), F32),
            pltpu.VMEM((peers, 1, tokens), jnp.int32),
            pltpu.VMEM((peers, 1, tokens), jnp.int32),
            pltpu.VMEM((1, length), F32),
            pltpu.VMEM((1, length), F32),
            pltpu.VMEM((length, LANES), F32),
            pltpu.VMEM((length, LANES), F32),
            pltpu.VMEM((tokens, features), BF16),
            pltpu.VMEM((tokens, features), BF16),
            pltpu.VMEM((peers, 8, tokens), F32),
            pltpu.VMEM((peers, 8, tokens), F32),
            pltpu.VMEM((heads, 1, length), F32),
            dma((7, heads)), dma((7, heads)),
            dma, dma((heads,)),
            dma, dma,
            dma((3,)), dma((3, heads)),
            dma((2,)), dma((2,)),
            dma, dma,
            dma, dma,
            dma((2,)),
        ],
        compiler_params=pltpu.CompilerParams(
            collective_id=0, has_side_effects=True, vmem_limit_bytes=62 << 20
        ),
    )(
        flat(new_input), flat(new_query), flat(new_key), flat(new_value),
        flat(old_query), flat(old_key), flat(old_value), flat(old_output), flat(old_cotangent),
        new_modality.reshape(1, tokens), old_modality.reshape(1, tokens), cross_bias,
    )
    summed = (shifted.astype(F32) + att.astype(F32)).astype(BF16)

    def whole(x):
        return x[None, None]

    return whole(summed), whole(dq), whole(dk), whole(dv), db[:1, :heads]


def solution(mesh):
    tokens = P("section", "dp", "ctx", None)
    flags = P("section", "dp", "ctx")
    biases = P("section", "ctx")
    return jax.shard_map(
        shards,
        mesh=mesh,
        in_specs=(tokens,) * 4 + (flags,) + (tokens,) * 5 + (flags, biases),
        out_specs=(tokens,) * 4 + (biases,),
        check_vma=False,
    )
```

```python
import functools

import jax
import jax.numpy as jnp
from jax import lax
from jax.experimental import pallas as pl
from jax.experimental.pallas import tpu as pltpu
from jax.sharding import PartitionSpec as P

MESH = pl.DeviceIdType.MESH
NT = (((1,), (1,)), ((), ()))
TN = (((0,), (0,)), ((), ()))
F32 = jnp.float32
BF16 = jnp.bfloat16
NEG = -1e30
LOG2E = 1.4426950408889634
LANES = 128


def forward_block(i, bq, q_ref, k_ref, v_ref, o_ref, row_ref, col_ref, bias):
    length, width = k_ref.shape
    c1 = width**-0.5 * LOG2E
    rows = pl.ds(pl.multiple_of(i * bq, bq), bq)
    scores = lax.dot_general(q_ref[rows, :], k_ref[...], NT, preferred_element_type=F32)
    traj = col_ref[rows, :] > 0.5
    logits, top = [], None
    for c in range(length // LANES):
        cols = slice(c * LANES, (c + 1) * LANES)
        key_traj = row_ref[:, cols]
        yes = (1.0 - key_traj) * (bias * LOG2E)
        no = key_traj * NEG
        x = scores[:, cols] * c1 + jnp.where(traj, yes, no)
        logits.append(x)
        top = x if top is None else jnp.maximum(top, x)
    top = jnp.max(top, axis=1, keepdims=True)
    total, weights = None, []
    for x in logits:
        p = jnp.exp2(x - top)
        total = p if total is None else total + p
        weights.append(p.astype(BF16))
    total = jnp.sum(total, axis=1, keepdims=True)
    out = jnp.dot(jnp.concatenate(weights, axis=1), v_ref[...], preferred_element_type=F32)
    o_ref[rows, :] = (out / total).astype(BF16)


def backward_block(
    i, bq, bk, q_ref, k_ref, v_ref, do_ref, dq_ref, dk_acc, dv_acc, x_scr, ds_scr, b_acc, row_ref, col_ref, del_ref, bias
):
    length, width = k_ref.shape
    scale = width**-0.5
    c1 = scale * LOG2E
    rows = pl.ds(pl.multiple_of(i * bq, bq), bq)
    q = q_ref[rows, :]
    do = do_ref[rows, :]
    traj = row_ref[:, rows]
    yes = traj * (bias * LOG2E)
    no = (1.0 - traj) * NEG
    delta = del_ref[:, rows]
    blocks = [slice(c * bk, (c + 1) * bk) for c in range(length // bk)]

    def video(ks):
        return jnp.concatenate([col_ref[ks, :]] * (bq // LANES), axis=1) < 0.5

    def fold(x):
        return x.reshape(bk // 8, 8, bq)

    top = None
    for ks in blocks:
        s = lax.dot_general(k_ref[ks, :], q, NT, preferred_element_type=F32)
        x = s * c1 + jnp.where(video(ks), yes, no)
        x_scr[ks, :] = x
        t = jnp.max(fold(x), axis=0)
        top = t if top is None else jnp.maximum(top, t)
    top = jnp.max(top, axis=0, keepdims=True)
    total = None
    for ks in blocks:
        p = jnp.exp2(x_scr[ks, :] - top)
        x_scr[ks, :] = p
        t = jnp.sum(fold(p), axis=0)
        total = t if total is None else total + t
    inverse = 1.0 / jnp.sum(total, axis=0, keepdims=True)
    b_sum = None
    for ks in blocks:
        dp = lax.dot_general(v_ref[ks, :], do, NT, preferred_element_type=F32)
        p = x_scr[ks, :] * inverse
        ds = p * (dp - delta)
        t = jnp.sum(fold(jnp.where(video(ks), ds, 0.0)), axis=0)
        b_sum = t if b_sum is None else b_sum + t
        low = ds.astype(BF16)
        ds_scr[ks, :] = low
        dv_acc[ks, :] += jnp.dot(p.astype(BF16), do, preferred_element_type=F32)
        dk_acc[ks, :] += jnp.dot(low, q, preferred_element_type=F32)
    b_acc[...] += b_sum * traj
    dq = lax.dot_general(ds_scr[...], k_ref[...], TN, preferred_element_type=F32)
    dq_ref[rows, :] = (dq * scale).astype(BF16)


def body(
    heads, bqf, bq, bk,
    ni, nq, nk, nv, oq, ok, ov, oo, oc, nm, om, bias,
    next_out, dq_out, dk_out, dv_out, db_out,
    new_buf, old_buf, ni_buf, att, grads, dk_acc, dv_acc, x_scr, ds_scr, b_acc, b_row, db_s, db_r,
    mod_n, mod_o, row_n, row_o, col_n, col_o, c_buf, o_buf, del_s, del_r, del_rows,
    in_recv, in_send, att_recv, att_send, g_recv, g_send,
    mod_recv, mod_send, del_recv, del_send, db_recv, db_send, loc_sem,
):
    peers = lax.axis_size("ctx")
    sections = lax.axis_size("section")
    replicas = lax.axis_size("dp")
    me = lax.axis_index("ctx")
    section = lax.axis_index("section")
    replica = lax.axis_index("dp")
    next_section = (section + 1) % sections
    tokens = nq.shape[0]
    width = new_buf.shape[3]
    length = new_buf.shape[2]
    my_rows = pl.ds(pl.multiple_of(me * tokens, tokens), tokens)
    whole = pl.ds(0, (peers - 1) * tokens)

    def head_cols(p, h):
        return pl.ds(pl.multiple_of((p * heads + h) * width, width), width)

    def token_rows(p):
        return pl.ds(pl.multiple_of(p * tokens, tokens), tokens)

    barrier = pltpu.get_barrier_semaphore()

    @pl.loop(1, peers)
    def _(k):
        pl.semaphore_signal(barrier, inc=1, device_id={"ctx": (me + k) % peers}, device_id_type=MESH)

    @pl.loop(0, peers)
    def _(k):
        pl.semaphore_signal(barrier, inc=1, device_id={"section": next_section, "ctx": k}, device_id_type=MESH)

    @pl.loop(1, replicas)
    def _(k):
        pl.semaphore_signal(barrier, inc=1, device_id={"dp": (replica + k) % replicas}, device_id_type=MESH)

    pl.semaphore_wait(barrier, 2 * peers - 1 + replicas - 1)

    load_c = pltpu.make_async_copy(oc, c_buf, loc_sem.at[0])
    load_o = pltpu.make_async_copy(oo, o_buf, loc_sem.at[1])
    for ref, buf, j in ((nm, mod_n, 0), (om, mod_o, 1)):
        pltpu.make_async_copy(ref, buf.at[me], mod_recv.at[j]).start()

        @pl.loop(1, peers)
        def _(k):
            pltpu.make_async_remote_copy(
                src_ref=ref, dst_ref=buf.at[me], send_sem=mod_send.at[j], recv_sem=mod_recv.at[j],
                device_id={"ctx": (me + k) % peers}, device_id_type=MESH,
            ).start()

    def send_in(arrays, buf, first, start, stop):
        @pl.loop(start, stop)
        def _(h):
            for a, src in enumerate(arrays):
                pltpu.make_async_copy(
                    src.at[:, head_cols(me, h)], buf.at[a, h, my_rows, :], in_recv.at[first + a, h]
                ).start()

                @pl.loop(1, peers)
                def _(k):
                    t = (me + k) % peers
                    pltpu.make_async_remote_copy(
                        src_ref=src.at[:, head_cols(t, h)], dst_ref=buf.at[a, h, my_rows, :],
                        send_sem=in_send.at[first + a, h], recv_sem=in_recv.at[first + a, h],
                        device_id={"ctx": t}, device_id_type=MESH,
                    ).start()

    send_in((nq, nk, nv), new_buf, 0, 0, heads)
    load_c.start()
    load_o.start()
    load_c.wait()
    load_o.wait()

    @pl.loop(0, peers)
    def _(p):
        for j in range(heads):
            cols = head_cols(p, j)
            prod = c_buf[:, cols].astype(F32) * o_buf[:, cols].astype(F32)
            del_s[p, j : j + 1, :] = jnp.sum(prod.T, axis=0, keepdims=True)

    for buf, row, col, j in ((mod_n, row_n, col_n, 0), (mod_o, row_o, col_o, 1)):
        pltpu.make_async_copy(buf, buf, mod_recv.at[j]).wait()
        for c in range(peers):
            flags = (buf[c] == 1).astype(F32)
            row[:, c * tokens : (c + 1) * tokens] = flags
            col[c * tokens : (c + 1) * tokens, :] = jnp.broadcast_to(flags, (LANES, tokens)).T

    pltpu.make_async_copy(del_s.at[me], del_r.at[me], del_recv).start()

    @pl.loop(1, peers)
    def _(k):
        t = (me + k) % peers
        pltpu.make_async_remote_copy(
            src_ref=del_s.at[t], dst_ref=del_r.at[me], send_sem=del_send, recv_sem=del_recv,
            device_id={"ctx": t}, device_id_type=MESH,
        ).start()

    send_in((oq, ok, ov, oc), old_buf, 3, 0, heads - 1)
    send_in((ni,), ni_buf, 7, 0, heads)
    send_in((oq, ok, ov, oc), old_buf, 3, heads - 1, heads)

    def wait_in(buf, a, first, h):
        pltpu.make_async_copy(buf.at[a, h], buf.at[a, h], in_recv.at[first + a, h]).wait()

    @pl.loop(0, heads)
    def _(h):
        for a in range(3):
            wait_in(new_buf, a, 0, h)
        limit = bias[0, h]

        @pl.loop(0, length // bqf)
        def _(i):
            forward_block(
                i, bqf, new_buf.at[0, h], new_buf.at[1, h], new_buf.at[2, h], att.at[h], row_n, col_n, limit
            )

    pltpu.make_async_copy(del_r, del_r, del_recv).wait()
    for c in range(peers):
        for j in range(heads):
            del_rows[j, :, c * tokens : (c + 1) * tokens] = del_r[c, j : j + 1, :]

    def residual():
        @pl.loop(0, heads)
        def _(h):
            wait_in(ni_buf, 0, 7, h)

            @pl.loop(0, length // bqf)
            def _(i):
                rows = pl.ds(pl.multiple_of(i * bqf, bqf), bqf)
                att[h, rows, :] = (ni_buf[0, h, rows, :].astype(F32) + att[h, rows, :].astype(F32)).astype(BF16)

        @pl.loop(0, heads)
        def _(h):
            @pl.loop(0, peers)
            def _(k):
                t = (me + k) % peers
                pltpu.make_async_remote_copy(
                    src_ref=att.at[h, token_rows(t), :], dst_ref=next_out.at[:, head_cols(me, h)],
                    send_sem=att_send.at[h], recv_sem=att_recv,
                    device_id={"section": next_section, "ctx": t}, device_id_type=MESH,
                ).start()

    b_row[...] = jnp.zeros_like(b_row)
    lane = lax.broadcasted_iota(jnp.int32, (8, LANES), 1)

    @pl.loop(0, heads)
    def _(h):
        for a in range(4):
            wait_in(old_buf, a, 3, h)
        limit = bias[0, h]
        dk_acc[...] = jnp.zeros_like(dk_acc)
        dv_acc[...] = jnp.zeros_like(dv_acc)
        b_acc[...] = jnp.zeros_like(b_acc)

        @pl.loop(0, length // bq)
        def _(i):
            backward_block(
                i, bq, bk, old_buf.at[0, h], old_buf.at[1, h], old_buf.at[2, h], old_buf.at[3, h],
                grads.at[0, h], dk_acc, dv_acc, x_scr, ds_scr, b_acc, row_o, col_o, del_rows.at[h], limit,
            )

        @pl.when(h == heads - 2)
        def _():
            residual()

        grads[1, h] = (dk_acc[...] * width**-0.5).astype(BF16)
        grads[2, h] = dv_acc[...].astype(BF16)
        share = jnp.sum(jnp.sum(b_acc[...], axis=0, keepdims=True), axis=1, keepdims=True)
        b_row[...] += jnp.where(lane == h, share, 0.0)
        for g, out in enumerate((dq_out, dk_out, dv_out)):
            pltpu.make_async_copy(grads.at[g, h, my_rows, :], out.at[:, head_cols(me, h)], g_recv.at[g]).start()

            @pl.loop(1, peers)
            def _(k):
                t = (me + k) % peers
                pltpu.make_async_remote_copy(
                    src_ref=grads.at[g, h, token_rows(t), :], dst_ref=out.at[:, head_cols(me, h)],
                    send_sem=g_send.at[g, h], recv_sem=g_recv.at[g],
                    device_id={"ctx": t}, device_id_type=MESH,
                ).start()

    db_s[...] = b_row[...]

    def drain(ref, sem):
        pltpu.make_async_copy(ref, ref, sem).wait()

    for j, buf in enumerate((mod_n, mod_o)):
        drain(buf.at[pl.ds(0, peers - 1)], mod_send.at[j])
    drain(del_s.at[pl.ds(0, peers - 1)], del_send)

    @pl.loop(0, heads)
    def _(h):
        for a in range(3):
            drain(new_buf.at[a, h, whole, :], in_send.at[a, h])
        for a in range(4):
            drain(old_buf.at[a, h, whole, :], in_send.at[3 + a, h])
        drain(ni_buf.at[0, h, whole, :], in_send.at[7, h])

    pltpu.make_async_copy(db_s, db_r.at[replica], db_recv).start()

    @pl.loop(1, replicas)
    def _(k):
        pltpu.make_async_remote_copy(
            src_ref=db_s, dst_ref=db_r.at[replica], send_sem=db_send, recv_sem=db_recv,
            device_id={"dp": (replica + k) % replicas}, device_id_type=MESH,
        ).start()

    @pl.loop(0, heads)
    def _(h):
        drain(att.at[h], att_send.at[h])
        for g in range(3):
            drain(grads.at[g, h, whole, :], g_send.at[g, h])

    pltpu.make_async_copy(db_r, db_r, db_recv).wait()
    acc = db_r[0]
    for r in range(1, replicas):
        acc = acc + db_r[r]
    db_out[...] = acc
    drain(db_r.at[pl.ds(0, replicas - 1)], db_send)
    drain(next_out, att_recv)
    for g, out in enumerate((dq_out, dk_out, dv_out)):
        drain(out, g_recv.at[g])


def shards(
    new_input, new_query, new_key, new_value, new_modality,
    old_query, old_key, old_value, old_output, old_cotangent, old_modality, cross_bias,
):
    tokens, features = new_query.shape[2:]
    heads = cross_bias.shape[1]
    peers = lax.axis_size("ctx")
    replicas = lax.axis_size("dp")
    length = tokens * peers
    width = features // (heads * peers)
    bqf, bq, bk = 256, 256, 256

    def flat(x):
        return x.reshape(x.shape[-2:])

    full = jax.ShapeDtypeStruct((tokens, features), BF16)
    dma = pltpu.SemaphoreType.DMA
    any_spec = pl.BlockSpec(memory_space=pl.ANY)
    following, dq, dk, dv, db = pl.pallas_call(
        functools.partial(body, heads, bqf, bq, bk),
        out_shape=[full] * 4 + [jax.ShapeDtypeStruct((8, LANES), F32)],
        in_specs=[any_spec] * 11 + [pl.BlockSpec(memory_space=pltpu.SMEM)],
        out_specs=[any_spec] * 4 + [pl.BlockSpec(memory_space=pltpu.VMEM)],
        scratch_shapes=[
            pltpu.VMEM((3, heads, length, width), BF16),
            pltpu.VMEM((4, heads, length, width), BF16),
            pltpu.VMEM((1, heads, length, width), BF16),
            pltpu.VMEM((heads, length, width), BF16),
            pltpu.VMEM((3, heads, length, width), BF16),
            pltpu.VMEM((length, width), F32),
            pltpu.VMEM((length, width), F32),
            pltpu.VMEM((length, bq), F32),
            pltpu.VMEM((length, bq), BF16),
            pltpu.VMEM((8, bq), F32),
            pltpu.VMEM((8, LANES), F32),
            pltpu.VMEM((8, LANES), F32),
            pltpu.VMEM((replicas, 8, LANES), F32),
            pltpu.VMEM((peers, 1, tokens), jnp.int32),
            pltpu.VMEM((peers, 1, tokens), jnp.int32),
            pltpu.VMEM((1, length), F32),
            pltpu.VMEM((1, length), F32),
            pltpu.VMEM((length, LANES), F32),
            pltpu.VMEM((length, LANES), F32),
            pltpu.VMEM((tokens, features), BF16),
            pltpu.VMEM((tokens, features), BF16),
            pltpu.VMEM((peers, 8, tokens), F32),
            pltpu.VMEM((peers, 8, tokens), F32),
            pltpu.VMEM((heads, 1, length), F32),
            dma((8, heads)), dma((8, heads)),
            dma, dma((heads,)),
            dma((3,)), dma((3, heads)),
            dma((2,)), dma((2,)),
            dma, dma,
            dma, dma,
            dma((2,)),
        ],
        compiler_params=pltpu.CompilerParams(
            collective_id=0, has_side_effects=True, vmem_limit_bytes=62 << 20
        ),
    )(
        flat(new_input), flat(new_query), flat(new_key), flat(new_value),
        flat(old_query), flat(old_key), flat(old_value), flat(old_output), flat(old_cotangent),
        new_modality.reshape(1, tokens), old_modality.reshape(1, tokens), cross_bias,
    )

    def whole(x):
        return x[None, None]

    return whole(following), whole(dq), whole(dk), whole(dv), db[:1, :heads]


def solution(mesh):
    tokens = P("section", "dp", "ctx", None)
    flags = P("section", "dp", "ctx")
    biases = P("section", "ctx")
    return jax.shard_map(
        shards,
        mesh=mesh,
        in_specs=(tokens,) * 4 + (flags,) + (tokens,) * 5 + (flags, biases),
        out_specs=(tokens,) * 4 + (biases,),
        check_vma=False,
    )
```

```python
import functools

import jax
import jax.numpy as jnp
from jax import lax
from jax.experimental import pallas as pl
from jax.experimental.pallas import tpu as pltpu
from jax.sharding import PartitionSpec as P

MESH = pl.DeviceIdType.MESH
NT = (((1,), (1,)), ((), ()))
TN = (((0,), (0,)), ((), ()))
F32 = jnp.float32
BF16 = jnp.bfloat16
NEG = -1e30
LOG2E = 1.4426950408889634
LANES = 128


def forward_block(i, bq, q_ref, k_ref, v_ref, o_ref, row_ref, col_ref, bias):
    length, width = k_ref.shape
    c1 = width**-0.5 * LOG2E
    rows = pl.ds(pl.multiple_of(i * bq, bq), bq)
    scores = lax.dot_general(q_ref[rows, :], k_ref[...], NT, preferred_element_type=F32)
    traj = col_ref[rows, :] > 0.5
    logits, top = [], None
    for c in range(length // LANES):
        cols = slice(c * LANES, (c + 1) * LANES)
        key_traj = row_ref[:, cols]
        yes = (1.0 - key_traj) * (bias * LOG2E)
        no = key_traj * NEG
        x = scores[:, cols] * c1 + jnp.where(traj, yes, no)
        logits.append(x)
        top = x if top is None else jnp.maximum(top, x)
    top = jnp.max(top, axis=1, keepdims=True)
    total, weights = None, []
    for x in logits:
        p = jnp.exp2(x - top)
        total = p if total is None else total + p
        weights.append(p.astype(BF16))
    total = jnp.sum(total, axis=1, keepdims=True)
    out = jnp.dot(jnp.concatenate(weights, axis=1), v_ref[...], preferred_element_type=F32)
    o_ref[rows, :] = (out / total).astype(BF16)


def backward_block(
    i, bq, bk, q_ref, k_ref, v_ref, do_ref, dq_ref, dk_acc, dv_acc, x_scr, ds_scr, b_acc, row_ref, col_ref, del_ref, bias
):
    length, width = k_ref.shape
    scale = width**-0.5
    c1 = scale * LOG2E
    rows = pl.ds(pl.multiple_of(i * bq, bq), bq)
    q = q_ref[rows, :]
    do = do_ref[rows, :]
    traj = row_ref[:, rows]
    yes = traj * (bias * LOG2E)
    no = (1.0 - traj) * NEG
    delta = del_ref[:, rows]
    blocks = [slice(c * bk, (c + 1) * bk) for c in range(length // bk)]

    def video(ks):
        return jnp.concatenate([col_ref[ks, :]] * (bq // LANES), axis=1) < 0.5

    def fold(x):
        return x.reshape(bk // 8, 8, bq)

    top = None
    for ks in blocks:
        s = lax.dot_general(k_ref[ks, :], q, NT, preferred_element_type=F32)
        x = s * c1 + jnp.where(video(ks), yes, no)
        x_scr[ks, :] = x
        t = jnp.max(fold(x), axis=0)
        top = t if top is None else jnp.maximum(top, t)
    top = jnp.max(top, axis=0, keepdims=True)
    total = None
    for ks in blocks:
        p = jnp.exp2(x_scr[ks, :] - top)
        x_scr[ks, :] = p
        t = jnp.sum(fold(p), axis=0)
        total = t if total is None else total + t
    inverse = 1.0 / jnp.sum(total, axis=0, keepdims=True)
    b_sum = None
    for ks in blocks:
        dp = lax.dot_general(v_ref[ks, :], do, NT, preferred_element_type=F32)
        p = x_scr[ks, :] * inverse
        ds = p * (dp - delta)
        t = jnp.sum(fold(jnp.where(video(ks), ds, 0.0)), axis=0)
        b_sum = t if b_sum is None else b_sum + t
        low = ds.astype(BF16)
        ds_scr[ks, :] = low
        dv_acc[ks, :] += jnp.dot(p.astype(BF16), do, preferred_element_type=F32)
        dk_acc[ks, :] += jnp.dot(low, q, preferred_element_type=F32)
    b_acc[...] += b_sum * traj
    dq = lax.dot_general(ds_scr[...], k_ref[...], TN, preferred_element_type=F32)
    dq_ref[rows, :] = (dq * scale).astype(BF16)


def body(
    heads, bqf, bq, bk,
    ni, nq, nk, nv, oq, ok, ov, oo, oc, nm, om, bias,
    next_out, dq_out, dk_out, dv_out, db_out,
    new_buf, old_buf, ni_buf, att, grads, dk_acc, dv_acc, x_scr, ds_scr, b_acc, b_row, db_s, db_r,
    mod_n, mod_o, row_n, row_o, col_n, col_o, c_buf, o_buf, del_s, del_r, del_rows,
    in_recv, in_send, att_recv, att_send, g_recv, g_send,
    mod_recv, mod_send, del_recv, del_send, db_recv, db_send, loc_sem,
):
    peers = lax.axis_size("ctx")
    sections = lax.axis_size("section")
    replicas = lax.axis_size("dp")
    me = lax.axis_index("ctx")
    section = lax.axis_index("section")
    replica = lax.axis_index("dp")
    next_section = (section + 1) % sections
    tokens = nq.shape[0]
    width = new_buf.shape[3]
    length = new_buf.shape[2]
    my_rows = pl.ds(pl.multiple_of(me * tokens, tokens), tokens)
    whole = pl.ds(0, (peers - 1) * tokens)

    def head_cols(p, h):
        return pl.ds(pl.multiple_of((p * heads + h) * width, width), width)

    def token_rows(p):
        return pl.ds(pl.multiple_of(p * tokens, tokens), tokens)

    barrier = pltpu.get_barrier_semaphore()

    @pl.loop(1, peers)
    def _(k):
        pl.semaphore_signal(barrier, inc=1, device_id={"ctx": (me + k) % peers}, device_id_type=MESH)

    @pl.loop(0, peers)
    def _(k):
        pl.semaphore_signal(barrier, inc=1, device_id={"section": next_section, "ctx": k}, device_id_type=MESH)

    @pl.loop(1, replicas)
    def _(k):
        pl.semaphore_signal(barrier, inc=1, device_id={"dp": (replica + k) % replicas}, device_id_type=MESH)

    pl.semaphore_wait(barrier, 2 * peers - 1 + replicas - 1)

    load_c = pltpu.make_async_copy(oc, c_buf, loc_sem.at[0])
    load_o = pltpu.make_async_copy(oo, o_buf, loc_sem.at[1])
    for ref, buf, j in ((nm, mod_n, 0), (om, mod_o, 1)):
        pltpu.make_async_copy(ref, buf.at[me], mod_recv.at[j]).start()

        @pl.loop(1, peers)
        def _(k):
            pltpu.make_async_remote_copy(
                src_ref=ref, dst_ref=buf.at[me], send_sem=mod_send.at[j], recv_sem=mod_recv.at[j],
                device_id={"ctx": (me + k) % peers}, device_id_type=MESH,
            ).start()

    def send_in(arrays, buf, first, start, stop):
        @pl.loop(start, stop)
        def _(h):
            for a, src in enumerate(arrays):
                pltpu.make_async_copy(
                    src.at[:, head_cols(me, h)], buf.at[a, h, my_rows, :], in_recv.at[first + a, h]
                ).start()

                @pl.loop(1, peers)
                def _(k):
                    t = (me + k) % peers
                    pltpu.make_async_remote_copy(
                        src_ref=src.at[:, head_cols(t, h)], dst_ref=buf.at[a, h, my_rows, :],
                        send_sem=in_send.at[first + a, h], recv_sem=in_recv.at[first + a, h],
                        device_id={"ctx": t}, device_id_type=MESH,
                    ).start()

    send_in((nq, nk, nv), new_buf, 0, 0, heads)
    load_c.start()
    load_o.start()
    load_c.wait()
    load_o.wait()

    @pl.loop(0, peers)
    def _(p):
        for j in range(heads):
            cols = head_cols(p, j)
            prod = c_buf[:, cols].astype(F32) * o_buf[:, cols].astype(F32)
            del_s[p, j : j + 1, :] = jnp.sum(prod.T, axis=0, keepdims=True)

    for buf, row, col, j in ((mod_n, row_n, col_n, 0), (mod_o, row_o, col_o, 1)):
        pltpu.make_async_copy(buf, buf, mod_recv.at[j]).wait()
        for c in range(peers):
            flags = (buf[c] == 1).astype(F32)
            row[:, c * tokens : (c + 1) * tokens] = flags
            col[c * tokens : (c + 1) * tokens, :] = jnp.broadcast_to(flags, (LANES, tokens)).T

    pltpu.make_async_copy(del_s.at[me], del_r.at[me], del_recv).start()

    @pl.loop(1, peers)
    def _(k):
        t = (me + k) % peers
        pltpu.make_async_remote_copy(
            src_ref=del_s.at[t], dst_ref=del_r.at[me], send_sem=del_send, recv_sem=del_recv,
            device_id={"ctx": t}, device_id_type=MESH,
        ).start()

    send_in((oq, ok, ov, oc), old_buf, 3, 0, 1)
    send_in((ni,), ni_buf, 7, 0, heads)
    send_in((oq, ok, ov, oc), old_buf, 3, 1, heads)

    def wait_in(buf, a, first, h):
        pltpu.make_async_copy(buf.at[a, h], buf.at[a, h], in_recv.at[first + a, h]).wait()

    @pl.loop(0, heads)
    def _(h):
        for a in range(3):
            wait_in(new_buf, a, 0, h)
        limit = bias[0, h]

        @pl.loop(0, length // bqf)
        def _(i):
            forward_block(
                i, bqf, new_buf.at[0, h], new_buf.at[1, h], new_buf.at[2, h], att.at[h], row_n, col_n, limit
            )

    pltpu.make_async_copy(del_r, del_r, del_recv).wait()
    for c in range(peers):
        for j in range(heads):
            del_rows[j, :, c * tokens : (c + 1) * tokens] = del_r[c, j : j + 1, :]

    def residual(h):
        wait_in(ni_buf, 0, 7, h)

        @pl.loop(0, length // bqf)
        def _(i):
            rows = pl.ds(pl.multiple_of(i * bqf, bqf), bqf)
            att[h, rows, :] = (ni_buf[0, h, rows, :].astype(F32) + att[h, rows, :].astype(F32)).astype(BF16)

    def send_next(h, t):
        pltpu.make_async_remote_copy(
            src_ref=att.at[h, token_rows(t), :], dst_ref=next_out.at[:, head_cols(me, h)],
            send_sem=att_send.at[h], recv_sem=att_recv,
            device_id={"section": next_section, "ctx": t}, device_id_type=MESH,
        ).start()

    b_row[...] = jnp.zeros_like(b_row)
    lane = lax.broadcasted_iota(jnp.int32, (8, LANES), 1)

    @pl.loop(0, heads)
    def _(h):
        for a in range(4):
            wait_in(old_buf, a, 3, h)
        limit = bias[0, h]
        dk_acc[...] = jnp.zeros_like(dk_acc)
        dv_acc[...] = jnp.zeros_like(dv_acc)
        b_acc[...] = jnp.zeros_like(b_acc)

        @pl.loop(0, length // bq)
        def _(i):
            backward_block(
                i, bq, bk, old_buf.at[0, h], old_buf.at[1, h], old_buf.at[2, h], old_buf.at[3, h],
                grads.at[0, h], dk_acc, dv_acc, x_scr, ds_scr, b_acc, row_o, col_o, del_rows.at[h], limit,
            )

        residual(h)
        grads[1, h] = (dk_acc[...] * width**-0.5).astype(BF16)
        grads[2, h] = dv_acc[...].astype(BF16)
        share = jnp.sum(jnp.sum(b_acc[...], axis=0, keepdims=True), axis=1, keepdims=True)
        b_row[...] += jnp.where(lane == h, share, 0.0)
        for g, out in enumerate((dq_out, dk_out, dv_out)):
            pltpu.make_async_copy(grads.at[g, h, my_rows, :], out.at[:, head_cols(me, h)], g_recv.at[g]).start()

            @pl.loop(1, peers)
            def _(k):
                t = (me + k) % peers
                pltpu.make_async_remote_copy(
                    src_ref=grads.at[g, h, token_rows(t), :], dst_ref=out.at[:, head_cols(me, h)],
                    send_sem=g_send.at[g, h], recv_sem=g_recv.at[g],
                    device_id={"ctx": t}, device_id_type=MESH,
                ).start()
                if g == 0:
                    send_next(h, (me + k + peers // 2) % peers)

            if g == 0:
                send_next(h, (me + peers // 2) % peers)

    db_s[...] = b_row[...]

    def drain(ref, sem):
        pltpu.make_async_copy(ref, ref, sem).wait()

    for j, buf in enumerate((mod_n, mod_o)):
        drain(buf.at[pl.ds(0, peers - 1)], mod_send.at[j])
    drain(del_s.at[pl.ds(0, peers - 1)], del_send)

    @pl.loop(0, heads)
    def _(h):
        for a in range(3):
            drain(new_buf.at[a, h, whole, :], in_send.at[a, h])
        for a in range(4):
            drain(old_buf.at[a, h, whole, :], in_send.at[3 + a, h])
        drain(ni_buf.at[0, h, whole, :], in_send.at[7, h])

    pltpu.make_async_copy(db_s, db_r.at[replica], db_recv).start()

    @pl.loop(1, replicas)
    def _(k):
        pltpu.make_async_remote_copy(
            src_ref=db_s, dst_ref=db_r.at[replica], send_sem=db_send, recv_sem=db_recv,
            device_id={"dp": (replica + k) % replicas}, device_id_type=MESH,
        ).start()

    @pl.loop(0, heads)
    def _(h):
        drain(att.at[h], att_send.at[h])
        for g in range(3):
            drain(grads.at[g, h, whole, :], g_send.at[g, h])

    pltpu.make_async_copy(db_r, db_r, db_recv).wait()
    acc = db_r[0]
    for r in range(1, replicas):
        acc = acc + db_r[r]
    db_out[...] = acc
    drain(db_r.at[pl.ds(0, replicas - 1)], db_send)
    drain(next_out, att_recv)
    for g, out in enumerate((dq_out, dk_out, dv_out)):
        drain(out, g_recv.at[g])


def hand_over(heads, chunks, *refs):
    count = (len(refs) - 3) // 2
    sources, db, targets, db_out = refs[:count], refs[count], refs[count + 1 : 2 * count + 1], refs[2 * count + 1]
    (sem,) = refs[2 * count + 2 :]
    step = sources[0].shape[0] // chunks

    def store(a, c):
        rows = pl.ds(c * step, step)
        return pltpu.make_async_copy(sources[a].at[rows, :], targets[a].at[rows, :], sem.at[a, c])

    pieces = [(a, c) for a in range(count) for c in range(chunks)]
    for piece in pieces:
        store(*piece).start()
    db_out[...] = db[:1, :heads]
    for piece in pieces:
        store(*piece).wait()


def shards(
    new_input, new_query, new_key, new_value, new_modality,
    old_query, old_key, old_value, old_output, old_cotangent, old_modality, cross_bias,
):
    tokens, features = new_query.shape[2:]
    heads = cross_bias.shape[1]
    peers = lax.axis_size("ctx")
    replicas = lax.axis_size("dp")
    length = tokens * peers
    width = features // (heads * peers)
    bqf, bq, bk = 256, 256, 256

    def flat(x):
        return x.reshape(x.shape[-2:])

    full = jax.ShapeDtypeStruct((tokens, features), BF16)
    dma = pltpu.SemaphoreType.DMA
    hbm_spec = pl.BlockSpec(memory_space=pltpu.HBM)
    vmem_spec = pl.BlockSpec(memory_space=pltpu.VMEM)
    following, dq, dk, dv, db = pl.pallas_call(
        functools.partial(body, heads, bqf, bq, bk),
        out_shape=[pltpu.VMEM((tokens, features), BF16)] * 4 + [pltpu.VMEM((8, LANES), F32)],
        in_specs=[hbm_spec] * 11 + [pl.BlockSpec(memory_space=pltpu.SMEM)],
        out_specs=[vmem_spec] * 5,
        scratch_shapes=[
            pltpu.VMEM((3, heads, length, width), BF16),
            pltpu.VMEM((4, heads, length, width), BF16),
            pltpu.VMEM((1, heads, length, width), BF16),
            pltpu.VMEM((heads, length, width), BF16),
            pltpu.VMEM((3, heads, length, width), BF16),
            pltpu.VMEM((length, width), F32),
            pltpu.VMEM((length, width), F32),
            pltpu.VMEM((length, bq), F32),
            pltpu.VMEM((length, bq), BF16),
            pltpu.VMEM((8, bq), F32),
            pltpu.VMEM((8, LANES), F32),
            pltpu.VMEM((8, LANES), F32),
            pltpu.VMEM((replicas, 8, LANES), F32),
            pltpu.VMEM((peers, 1, tokens), jnp.int32),
            pltpu.VMEM((peers, 1, tokens), jnp.int32),
            pltpu.VMEM((1, length), F32),
            pltpu.VMEM((1, length), F32),
            pltpu.VMEM((length, LANES), F32),
            pltpu.VMEM((length, LANES), F32),
            pltpu.VMEM((tokens, features), BF16),
            pltpu.VMEM((tokens, features), BF16),
            pltpu.VMEM((peers, 8, tokens), F32),
            pltpu.VMEM((peers, 8, tokens), F32),
            pltpu.VMEM((heads, 1, length), F32),
            dma((8, heads)), dma((8, heads)),
            dma, dma((heads,)),
            dma((3,)), dma((3, heads)),
            dma((2,)), dma((2,)),
            dma, dma,
            dma, dma,
            dma((2,)),
        ],
        compiler_params=pltpu.CompilerParams(
            collective_id=0, has_side_effects=True, vmem_limit_bytes=57 << 20
        ),
    )(
        flat(new_input), flat(new_query), flat(new_key), flat(new_value),
        flat(old_query), flat(old_key), flat(old_value), flat(old_output), flat(old_cotangent),
        new_modality.reshape(1, tokens), old_modality.reshape(1, tokens), cross_bias,
    )

    chunks = 4
    following, dq, dk, dv, db = pl.pallas_call(
        functools.partial(hand_over, heads, chunks),
        out_shape=[full] * 4 + [jax.ShapeDtypeStruct((1, heads), F32)],
        in_specs=[vmem_spec] * 5,
        out_specs=[hbm_spec] * 4 + [vmem_spec],
        scratch_shapes=[dma((4, chunks))],
        compiler_params=pltpu.CompilerParams(vmem_limit_bytes=30 << 20),
    )(following, dq, dk, dv, db)

    def whole(x):
        return x[None, None]

    return whole(following), whole(dq), whole(dk), whole(dv), db


def solution(mesh):
    tokens = P("section", "dp", "ctx", None)
    flags = P("section", "dp", "ctx")
    biases = P("section", "ctx")
    return jax.shard_map(
        shards,
        mesh=mesh,
        in_specs=(tokens,) * 4 + (flags,) + (tokens,) * 5 + (flags, biases),
        out_specs=(tokens,) * 4 + (biases,),
        check_vma=False,
    )
```

```python
import functools

import jax
import jax.numpy as jnp
from jax import lax
from jax.experimental import pallas as pl
from jax.experimental.pallas import tpu as pltpu
from jax.sharding import PartitionSpec as P

MESH = pl.DeviceIdType.MESH
NT = (((1,), (1,)), ((), ()))
TN = (((0,), (0,)), ((), ()))
F32 = jnp.float32
BF16 = jnp.bfloat16
NEG = -1e30
LOG2E = 1.4426950408889634
LANES = 128


def forward_block(i, bq, q_ref, k_ref, v_ref, o_ref, row_ref, col_ref, bias):
    length, width = k_ref.shape
    c1 = width**-0.5 * LOG2E
    rows = pl.ds(pl.multiple_of(i * bq, bq), bq)
    scores = lax.dot_general(q_ref[rows, :], k_ref[...], NT, preferred_element_type=F32)
    traj = col_ref[rows, :] > 0.5
    logits, top = [], None
    for c in range(length // LANES):
        cols = slice(c * LANES, (c + 1) * LANES)
        key_traj = row_ref[:, cols]
        yes = (1.0 - key_traj) * (bias * LOG2E)
        no = key_traj * NEG
        x = scores[:, cols] * c1 + jnp.where(traj, yes, no)
        logits.append(x)
        top = x if top is None else jnp.maximum(top, x)
    top = jnp.max(top, axis=1, keepdims=True)
    total, weights = None, []
    for x in logits:
        p = jnp.exp2(x - top)
        total = p if total is None else total + p
        weights.append(p.astype(BF16))
    total = jnp.sum(total, axis=1, keepdims=True)
    out = jnp.dot(jnp.concatenate(weights, axis=1), v_ref[...], preferred_element_type=F32)
    o_ref[rows, :] = (out / total).astype(BF16)


def backward_block(
    i, bq, bk, q_ref, k_ref, v_ref, do_ref, dq_ref, dk_acc, dv_acc, x_scr, ds_scr, b_acc, row_ref, col_ref, del_ref, bias
):
    length, width = k_ref.shape
    scale = width**-0.5
    c1 = scale * LOG2E
    rows = pl.ds(pl.multiple_of(i * bq, bq), bq)
    q = q_ref[rows, :]
    do = do_ref[rows, :]
    traj = row_ref[:, rows]
    yes = traj * (bias * LOG2E)
    no = (1.0 - traj) * NEG
    delta = del_ref[:, rows]
    blocks = [slice(c * bk, (c + 1) * bk) for c in range(length // bk)]

    def video(ks):
        return jnp.concatenate([col_ref[ks, :]] * (bq // LANES), axis=1) < 0.5

    def fold(x):
        return x.reshape(bk // 8, 8, bq)

    top = None
    for ks in blocks:
        s = lax.dot_general(k_ref[ks, :], q, NT, preferred_element_type=F32)
        x = s * c1 + jnp.where(video(ks), yes, no)
        x_scr[ks, :] = x
        t = jnp.max(fold(x), axis=0)
        top = t if top is None else jnp.maximum(top, t)
    top = jnp.max(top, axis=0, keepdims=True)
    total = None
    for ks in blocks:
        p = jnp.exp2(x_scr[ks, :] - top)
        x_scr[ks, :] = p
        t = jnp.sum(fold(p), axis=0)
        total = t if total is None else total + t
    inverse = 1.0 / jnp.sum(total, axis=0, keepdims=True)
    b_sum = None
    for ks in blocks:
        dp = lax.dot_general(v_ref[ks, :], do, NT, preferred_element_type=F32)
        p = x_scr[ks, :] * inverse
        ds = p * (dp - delta)
        t = jnp.sum(fold(jnp.where(video(ks), ds, 0.0)), axis=0)
        b_sum = t if b_sum is None else b_sum + t
        low = ds.astype(BF16)
        ds_scr[ks, :] = low
        dv_acc[ks, :] += jnp.dot(p.astype(BF16), do, preferred_element_type=F32)
        dk_acc[ks, :] += jnp.dot(low, q, preferred_element_type=F32)
    b_acc[...] += b_sum * traj
    dq = lax.dot_general(ds_scr[...], k_ref[...], TN, preferred_element_type=F32)
    dq_ref[rows, :] = (dq * scale).astype(BF16)


def body(
    heads, bqf, bq, bk,
    ni, nq, nk, nv, oq, ok, ov, oo, oc, nm, om, bias,
    next_out, dq_out, dk_out, dv_out, db_out,
    new_buf, old_buf, ni_buf, att, grads, dk_acc, dv_acc, x_scr, ds_scr, b_acc, b_row, db_s, db_r,
    mod_n, mod_o, row_n, row_o, col_n, col_o, c_buf, o_buf, del_s, del_r, del_rows,
    in_recv, in_send, att_recv, att_send, g_recv, g_send,
    mod_recv, mod_send, del_recv, del_send, db_recv, db_send, loc_sem,
):
    peers = lax.axis_size("ctx")
    sections = lax.axis_size("section")
    replicas = lax.axis_size("dp")
    me = lax.axis_index("ctx")
    section = lax.axis_index("section")
    replica = lax.axis_index("dp")
    next_section = (section + 1) % sections
    tokens = nq.shape[0]
    width = new_buf.shape[3]
    length = new_buf.shape[2]
    my_rows = pl.ds(pl.multiple_of(me * tokens, tokens), tokens)
    whole = pl.ds(0, (peers - 1) * tokens)

    def head_cols(p, h):
        return pl.ds(pl.multiple_of((p * heads + h) * width, width), width)

    def token_rows(p):
        return pl.ds(pl.multiple_of(p * tokens, tokens), tokens)

    barrier = pltpu.get_barrier_semaphore()

    @pl.loop(1, peers)
    def _(k):
        pl.semaphore_signal(barrier, inc=1, device_id={"ctx": (me + k) % peers}, device_id_type=MESH)

    @pl.loop(0, peers)
    def _(k):
        pl.semaphore_signal(barrier, inc=1, device_id={"section": next_section, "ctx": k}, device_id_type=MESH)

    @pl.loop(1, replicas)
    def _(k):
        pl.semaphore_signal(barrier, inc=1, device_id={"dp": (replica + k) % replicas}, device_id_type=MESH)

    pl.semaphore_wait(barrier, 2 * peers - 1 + replicas - 1)

    load_c = pltpu.make_async_copy(oc, c_buf, loc_sem.at[0])
    load_o = pltpu.make_async_copy(oo, o_buf, loc_sem.at[1])
    for ref, buf, j in ((nm, mod_n, 0), (om, mod_o, 1)):
        pltpu.make_async_copy(ref, buf.at[me], mod_recv.at[j]).start()

        @pl.loop(1, peers)
        def _(k):
            pltpu.make_async_remote_copy(
                src_ref=ref, dst_ref=buf.at[me], send_sem=mod_send.at[j], recv_sem=mod_recv.at[j],
                device_id={"ctx": (me + k) % peers}, device_id_type=MESH,
            ).start()

    def send_in(arrays, buf, first, start, stop):
        @pl.loop(start, stop)
        def _(h):
            for a, src in enumerate(arrays):
                pltpu.make_async_copy(
                    src.at[:, head_cols(me, h)], buf.at[a, h, my_rows, :], in_recv.at[first + a, h]
                ).start()

                @pl.loop(1, peers)
                def _(k):
                    t = (me + k) % peers
                    pltpu.make_async_remote_copy(
                        src_ref=src.at[:, head_cols(t, h)], dst_ref=buf.at[a, h, my_rows, :],
                        send_sem=in_send.at[first + a, h], recv_sem=in_recv.at[first + a, h],
                        device_id={"ctx": t}, device_id_type=MESH,
                    ).start()

    send_in((nq, nk, nv), new_buf, 0, 0, heads)
    load_c.start()
    load_o.start()
    load_c.wait()
    load_o.wait()

    @pl.loop(0, peers)
    def _(p):
        for j in range(heads):
            cols = head_cols(p, j)
            prod = c_buf[:, cols].astype(F32) * o_buf[:, cols].astype(F32)
            del_s[p, j : j + 1, :] = jnp.sum(prod.T, axis=0, keepdims=True)

    for buf, row, col, j in ((mod_n, row_n, col_n, 0), (mod_o, row_o, col_o, 1)):
        pltpu.make_async_copy(buf, buf, mod_recv.at[j]).wait()
        for c in range(peers):
            flags = (buf[c] == 1).astype(F32)
            row[:, c * tokens : (c + 1) * tokens] = flags
            col[c * tokens : (c + 1) * tokens, :] = jnp.broadcast_to(flags, (LANES, tokens)).T

    pltpu.make_async_copy(del_s.at[me], del_r.at[me], del_recv).start()

    @pl.loop(1, peers)
    def _(k):
        t = (me + k) % peers
        pltpu.make_async_remote_copy(
            src_ref=del_s.at[t], dst_ref=del_r.at[me], send_sem=del_send, recv_sem=del_recv,
            device_id={"ctx": t}, device_id_type=MESH,
        ).start()

    for h in range(heads):
        send_in((oq, ok, ov, oc), old_buf, 3, h, h + 1)
        send_in((ni,), ni_buf, 7, h, h + 1)

    def wait_in(buf, a, first, h):
        pltpu.make_async_copy(buf.at[a, h], buf.at[a, h], in_recv.at[first + a, h]).wait()

    @pl.loop(0, heads)
    def _(h):
        for a in range(3):
            wait_in(new_buf, a, 0, h)
        limit = bias[0, h]

        @pl.loop(0, length // bqf)
        def _(i):
            forward_block(
                i, bqf, new_buf.at[0, h], new_buf.at[1, h], new_buf.at[2, h], att.at[h], row_n, col_n, limit
            )

    pltpu.make_async_copy(del_r, del_r, del_recv).wait()
    for c in range(peers):
        for j in range(heads):
            del_rows[j, :, c * tokens : (c + 1) * tokens] = del_r[c, j : j + 1, :]

    def residual(h):
        wait_in(ni_buf, 0, 7, h)

        @pl.loop(0, length // bqf)
        def _(i):
            rows = pl.ds(pl.multiple_of(i * bqf, bqf), bqf)
            att[h, rows, :] = (ni_buf[0, h, rows, :].astype(F32) + att[h, rows, :].astype(F32)).astype(BF16)

    def send_next(h, t):
        pltpu.make_async_remote_copy(
            src_ref=att.at[h, token_rows(t), :], dst_ref=next_out.at[:, head_cols(me, h)],
            send_sem=att_send.at[h], recv_sem=att_recv,
            device_id={"section": next_section, "ctx": t}, device_id_type=MESH,
        ).start()

    b_row[...] = jnp.zeros_like(b_row)
    lane = lax.broadcasted_iota(jnp.int32, (8, LANES), 1)

    @pl.loop(0, heads)
    def _(h):
        for a in range(4):
            wait_in(old_buf, a, 3, h)
        limit = bias[0, h]
        dk_acc[...] = jnp.zeros_like(dk_acc)
        dv_acc[...] = jnp.zeros_like(dv_acc)
        b_acc[...] = jnp.zeros_like(b_acc)

        @pl.loop(0, length // bq)
        def _(i):
            backward_block(
                i, bq, bk, old_buf.at[0, h], old_buf.at[1, h], old_buf.at[2, h], old_buf.at[3, h],
                grads.at[0, h], dk_acc, dv_acc, x_scr, ds_scr, b_acc, row_o, col_o, del_rows.at[h], limit,
            )

        residual(h)
        grads[1, h] = (dk_acc[...] * width**-0.5).astype(BF16)
        grads[2, h] = dv_acc[...].astype(BF16)
        share = jnp.sum(jnp.sum(b_acc[...], axis=0, keepdims=True), axis=1, keepdims=True)
        b_row[...] += jnp.where(lane == h, share, 0.0)
        for g, out in enumerate((dq_out, dk_out, dv_out)):
            pltpu.make_async_copy(grads.at[g, h, my_rows, :], out.at[:, head_cols(me, h)], g_recv.at[g]).start()

            @pl.loop(1, peers)
            def _(k):
                t = (me + k) % peers
                pltpu.make_async_remote_copy(
                    src_ref=grads.at[g, h, token_rows(t), :], dst_ref=out.at[:, head_cols(me, h)],
                    send_sem=g_send.at[g, h], recv_sem=g_recv.at[g],
                    device_id={"ctx": t}, device_id_type=MESH,
                ).start()

                @pl.when(k % 3 == g)
                def _():
                    send_next(h, (me + k + peers // 2) % peers)

            if g == 0:
                send_next(h, (me + peers // 2) % peers)

    db_s[...] = b_row[...]

    def drain(ref, sem):
        pltpu.make_async_copy(ref, ref, sem).wait()

    for j, buf in enumerate((mod_n, mod_o)):
        drain(buf.at[pl.ds(0, peers - 1)], mod_send.at[j])
    drain(del_s.at[pl.ds(0, peers - 1)], del_send)

    @pl.loop(0, heads)
    def _(h):
        for a in range(3):
            drain(new_buf.at[a, h, whole, :], in_send.at[a, h])
        for a in range(4):
            drain(old_buf.at[a, h, whole, :], in_send.at[3 + a, h])
        drain(ni_buf.at[0, h, whole, :], in_send.at[7, h])

    pltpu.make_async_copy(db_s, db_r.at[replica], db_recv).start()

    @pl.loop(1, replicas)
    def _(k):
        pltpu.make_async_remote_copy(
            src_ref=db_s, dst_ref=db_r.at[replica], send_sem=db_send, recv_sem=db_recv,
            device_id={"dp": (replica + k) % replicas}, device_id_type=MESH,
        ).start()

    @pl.loop(0, heads)
    def _(h):
        drain(att.at[h], att_send.at[h])
        for g in range(3):
            drain(grads.at[g, h, whole, :], g_send.at[g, h])

    pltpu.make_async_copy(db_r, db_r, db_recv).wait()
    acc = db_r[0]
    for r in range(1, replicas):
        acc = acc + db_r[r]
    db_out[...] = acc
    drain(db_r.at[pl.ds(0, replicas - 1)], db_send)
    drain(next_out, att_recv)
    for g, out in enumerate((dq_out, dk_out, dv_out)):
        drain(out, g_recv.at[g])


def hand_over(heads, chunks, *refs):
    count = (len(refs) - 3) // 2
    sources, db, targets, db_out = refs[:count], refs[count], refs[count + 1 : 2 * count + 1], refs[2 * count + 1]
    (sem,) = refs[2 * count + 2 :]
    step = sources[0].shape[0] // chunks

    def store(a, c):
        rows = pl.ds(c * step, step)
        return pltpu.make_async_copy(sources[a].at[rows, :], targets[a].at[rows, :], sem.at[a, c])

    pieces = [(a, c) for a in range(count) for c in range(chunks)]
    for piece in pieces:
        store(*piece).start()
    db_out[...] = db[:1, :heads]
    for piece in pieces:
        store(*piece).wait()


def shards(
    new_input, new_query, new_key, new_value, new_modality,
    old_query, old_key, old_value, old_output, old_cotangent, old_modality, cross_bias,
):
    tokens, features = new_query.shape[2:]
    heads = cross_bias.shape[1]
    peers = lax.axis_size("ctx")
    replicas = lax.axis_size("dp")
    length = tokens * peers
    width = features // (heads * peers)
    bqf, bq, bk = 256, 256, 256

    def flat(x):
        return x.reshape(x.shape[-2:])

    full = jax.ShapeDtypeStruct((tokens, features), BF16)
    dma = pltpu.SemaphoreType.DMA
    hbm_spec = pl.BlockSpec(memory_space=pltpu.HBM)
    vmem_spec = pl.BlockSpec(memory_space=pltpu.VMEM)
    following, dq, dk, dv, db = pl.pallas_call(
        functools.partial(body, heads, bqf, bq, bk),
        out_shape=[pltpu.VMEM((tokens, features), BF16)] * 4 + [pltpu.VMEM((8, LANES), F32)],
        in_specs=[hbm_spec] * 11 + [pl.BlockSpec(memory_space=pltpu.SMEM)],
        out_specs=[vmem_spec] * 5,
        scratch_shapes=[
            pltpu.VMEM((3, heads, length, width), BF16),
            pltpu.VMEM((4, heads, length, width), BF16),
            pltpu.VMEM((1, heads, length, width), BF16),
            pltpu.VMEM((heads, length, width), BF16),
            pltpu.VMEM((3, heads, length, width), BF16),
            pltpu.VMEM((length, width), F32),
            pltpu.VMEM((length, width), F32),
            pltpu.VMEM((length, bq), F32),
            pltpu.VMEM((length, bq), BF16),
            pltpu.VMEM((8, bq), F32),
            pltpu.VMEM((8, LANES), F32),
            pltpu.VMEM((8, LANES), F32),
            pltpu.VMEM((replicas, 8, LANES), F32),
            pltpu.VMEM((peers, 1, tokens), jnp.int32),
            pltpu.VMEM((peers, 1, tokens), jnp.int32),
            pltpu.VMEM((1, length), F32),
            pltpu.VMEM((1, length), F32),
            pltpu.VMEM((length, LANES), F32),
            pltpu.VMEM((length, LANES), F32),
            pltpu.VMEM((tokens, features), BF16),
            pltpu.VMEM((tokens, features), BF16),
            pltpu.VMEM((peers, 8, tokens), F32),
            pltpu.VMEM((peers, 8, tokens), F32),
            pltpu.VMEM((heads, 1, length), F32),
            dma((8, heads)), dma((8, heads)),
            dma, dma((heads,)),
            dma((3,)), dma((3, heads)),
            dma((2,)), dma((2,)),
            dma, dma,
            dma, dma,
            dma((2,)),
        ],
        compiler_params=pltpu.CompilerParams(
            collective_id=0, has_side_effects=True, vmem_limit_bytes=57 << 20
        ),
    )(
        flat(new_input), flat(new_query), flat(new_key), flat(new_value),
        flat(old_query), flat(old_key), flat(old_value), flat(old_output), flat(old_cotangent),
        new_modality.reshape(1, tokens), old_modality.reshape(1, tokens), cross_bias,
    )

    chunks = 4
    following, dq, dk, dv, db = pl.pallas_call(
        functools.partial(hand_over, heads, chunks),
        out_shape=[full] * 4 + [jax.ShapeDtypeStruct((1, heads), F32)],
        in_specs=[vmem_spec] * 5,
        out_specs=[hbm_spec] * 4 + [vmem_spec],
        scratch_shapes=[dma((4, chunks))],
        compiler_params=pltpu.CompilerParams(vmem_limit_bytes=30 << 20),
    )(following, dq, dk, dv, db)

    def whole(x):
        return x[None, None]

    return whole(following), whole(dq), whole(dk), whole(dv), db


def solution(mesh):
    tokens = P("section", "dp", "ctx", None)
    flags = P("section", "dp", "ctx")
    biases = P("section", "ctx")
    return jax.shard_map(
        shards,
        mesh=mesh,
        in_specs=(tokens,) * 4 + (flags,) + (tokens,) * 5 + (flags, biases),
        out_specs=(tokens,) * 4 + (biases,),
        check_vma=False,
    )
```
